256 devices in a mesh: depth: 32 (over y, x, core), screen: 8 (over z).
Axes of the slice: x: 4, y: 4, z: 8, core: 2. Of those that a mesh axis runs over, the one named last changes fastest.
Arguments:
- density: bfloat16 [320, 768, 2048], P('depth', 'screen'), may hold values from 0.099609375 to 10
- material: int32 [256, 768, 2048], P('depth', 'screen'), may hold values from 0 to 15
- order: int32 [32], replicated, may hold values from 0 to 31, each once
- color_table: float32 [16, 3], replicated, may hold values from 0.3 to 3
- extinction: float32 [16], replicated, may hold values from 0.00390625 to 0.0390625
Outputs:
- image: float32 [4, 768, 2048], P(None, ('screen', 'depth'))
The draws below stay inside these ranges and needn't reach their ends.
Inputs may be any that keep to these rules, and one draw needn't show every extreme that they name: order is a permutation: each brick has a distinct rank.
All inputs are finite; a program needn't handle non-finite values.
Results may differ from the reference program's by a relative error of at most 0.0003.
Values may be sent and summed in bfloat16 or wider, within the bound.
No kernel may reach another device: no remote copies, remote signals or barrier semaphores. Data moves between devices by JAX's collectives and lax.ppermute only.
A program may use at most 128 MiB of HBM per device.

```python
import math
import jax
import jax.numpy as jnp
from jax import lax

NX = 2048
ZB = 8
NTF = 16
BRICKS = 32
NZ = 256
GZ = 320
NY = 768


def set_ends(array, key, low, top_value):
    longest = array.shape.index(max(array.shape))
    spots = []
    for shift in (0, 1):
        where = [jax.random.randint(jax.random.fold_in(key, axis), (), 0, length) for axis, length in enumerate(array.shape)]
        where[longest] = (where[longest] + shift) % array.shape[longest]
        spots.append(tuple(where))
    return array.at[spots[0]].set(low).at[spots[1]].set(top_value)


def block_levels(own_key, dims, shards, smallest, largest):
    loudness, own = 1.0, jax.random.fold_in(own_key, 6)
    for dim, shards_of in shards:
        draws = jnp.exp(jax.random.uniform(jax.random.fold_in(own, dim), (shards_of,), jnp.float32, smallest / len(shards), largest / len(shards)))
        loudness = loudness * jnp.repeat(draws, dims[dim] // shards_of).reshape([-1 if axis == dim else 1 for axis in range(len(dims))])
    return loudness


def setup_inputs(seed: int = 0) -> dict:
    keys = jax.random.split(jax.random.key(seed), 6)
    return {
        "density": jnp.clip(jnp.exp(math.log(10.0) - 4.609084 * jax.random.uniform(keys[0], (GZ, NY, NX), jnp.float32) ** block_levels(keys[0], (GZ, NY, NX), ((0, 32), (1, 8)), -0.2, 0.2)), 0.099609375, 10.0).astype(jnp.bfloat16),
        "material": set_ends(jax.random.randint(keys[1], (NZ, NY, NX), 0, NTF), jax.random.fold_in(keys[1], 1), 0, NTF - 1).astype(jnp.int32),
        "order": jax.random.permutation(keys[2], BRICKS).astype(jnp.int32),
        "color_table": jnp.clip(jnp.exp(jax.random.uniform(keys[3], (NTF, 3), jnp.float32, math.log(0.3), math.log(3.0))), 0.3, 3.0),
        "extinction": jnp.clip(jnp.exp(jax.random.uniform(keys[4], (NTF,), jnp.float32, math.log(0.00390625), math.log(0.0390625))), 0.00390625, 0.0390625),
    }


light_x = 0.48
light_y = 0.6
light_z = 0.64

def shade_brick(operands):
    block, kinds, color_table, extinction = operands
    full = block.astype(jnp.float32)
    padded = jnp.pad(full, ((0, 0), (1, 1), (1, 1)))
    grad_z = 0.5 * (full[2:] - full[:-2])
    grad_y = 0.5 * (padded[1:-1, 2:, 1:-1] - padded[1:-1, :-2, 1:-1])
    grad_x = 0.5 * (padded[1:-1, 1:-1, 2:] - padded[1:-1, 1:-1, :-2])
    lit = light_x * grad_x + light_y * grad_y + light_z * grad_z
    shade = 0.55 + 0.45 * lit / jnp.sqrt(1.0 + grad_x * grad_x + grad_y * grad_y + grad_z * grad_z)
    rho = full[1:-1]
    extinct = extinction[kinds] * (rho / (1.0 + rho))
    ahead = jnp.cumsum(extinct, axis=0) - extinct
    weight = jnp.exp(-ahead) * (1.0 - jnp.exp(-extinct)) * shade
    emitted = jnp.stack([lax.optimization_barrier(jnp.sum(weight * color_table[kinds, 0], axis=0)), lax.optimization_barrier(jnp.sum(weight * color_table[kinds, 1], axis=0)), lax.optimization_barrier(jnp.sum(weight * color_table[kinds, 2], axis=0))], axis=0)
    return (emitted, lax.optimization_barrier(jnp.sum(extinct, axis=0)))

def reference(density, material, order, color_table, extinction):
    blocks = density.reshape(BRICKS, ZB + 2, density.shape[1], density.shape[2])
    kinds = material.reshape(BRICKS, ZB, material.shape[1], material.shape[2])
    emitted, optical = lax.map(lambda pair: shade_brick((pair[0], pair[1], color_table, extinction)), (blocks, kinds))
    before = (order[None, :] < order[:, None]).astype(jnp.float32)
    front = jnp.einsum('kj,jyx->kyx', before, optical, precision=lax.Precision.HIGHEST)
    attenuate = jnp.exp(-front)
    colored = jnp.einsum('kcyx,kyx->cyx', emitted, attenuate, precision=lax.Precision.HIGHEST)
    opacity_total = 1.0 - jnp.exp(-lax.optimization_barrier(jnp.sum(optical, axis=0)))
    return jnp.concatenate([colored, opacity_total[None]], axis=0)
```

```python
import functools
import math

import jax
import jax.numpy as jnp
from jax import lax
from jax.experimental import pallas as pl
from jax.experimental.pallas import tpu as pltpu
from jax.sharding import PartitionSpec as P

light_x = 0.48
light_y = 0.6
light_z = 0.64
ambient = 0.55
diffuse = 0.45

LANES = 128
SUB = 8
CB = 256
PER = CB // LANES
LOG2E = math.log2(math.e)

SLICES = 8
TAU_TOP = SLICES * 0.0390625 * (10.0 / 11.0) * LOG2E * 1.001
LOG_TOP = 0.0
LOG_LOW = -14.0
LEVELS = 65535.0
TAU_STEP = TAU_TOP / LEVELS
LOG_STEP = (LOG_TOP - LOG_LOW) / LEVELS


def quantize(value, low, step):
    level = (value - low) * (1.0 / step) + 0.5
    return jnp.clip(level, 0.0, LEVELS).astype(jnp.int32)


def pick(low_table, high_table, index, upper):
    low = jnp.take_along_axis(low_table, index, axis=0)
    high = jnp.take_along_axis(high_table, index, axis=0)
    return jnp.where(upper, high, low)


def shade_kernel(blocks, left_ref, mid_ref, right_ref, low_ref, high_ref, mat_ref, tab_ref, band_ref, out_ref, full, diff):
    step = pl.program_id(0)
    ghost, rows = mid_ref.shape[0], mid_ref.shape[1]
    slices = ghost - 2
    for z in range(ghost):
        for c in range(PER):
            cols = pl.ds(c * LANES, LANES)
            full[z, c, SUB : SUB + rows, :] = mid_ref[z, :, cols].astype(jnp.float32)
            full[z, c, SUB - 1 : SUB, :] = low_ref[z, :, cols].astype(jnp.float32)
            full[z, c, SUB + rows : SUB + rows + 1, :] = high_ref[z, :, cols].astype(jnp.float32)
    window = jnp.concatenate([left_ref[1:-1], mid_ref[1:-1], right_ref[1:-1]], axis=-1)
    diff[...] = jnp.dot(
        window.reshape(slices * rows, CB + 2 * LANES), band_ref[0], preferred_element_type=jnp.float32
    ).reshape(slices, rows, CB)
    tables = [tab_ref[i] for i in range(8)]
    stride = 2 * blocks

    def row_block(r, carry):
        base = pl.multiple_of(r * SUB, SUB)
        for c in range(PER):
            cols = pl.ds(c * LANES, LANES)
            through = jnp.ones((SUB, LANES), jnp.float32)
            depth = jnp.zeros((SUB, LANES), jnp.float32)
            sums = [jnp.zeros((SUB, LANES), jnp.float32) for _ in range(3)]
            for z in range(slices):
                rho = full[z + 1, c, pl.ds(base + SUB, SUB), :]
                dz = full[z + 2, c, pl.ds(base + SUB, SUB), :] - full[z, c, pl.ds(base + SUB, SUB), :]
                dy = full[z + 1, c, pl.ds(base + SUB + 1, SUB), :] - full[z + 1, c, pl.ds(base + SUB - 1, SUB), :]
                dx = diff[z, pl.ds(base, SUB), cols]
                lit = (diffuse * light_x) * dx + (diffuse * light_y) * dy + (diffuse * light_z) * dz
                shade = ambient + lit * lax.rsqrt(4.0 + dx * dx + dy * dy + dz * dz)
                kind = mat_ref[z, pl.ds(base, SUB), cols]
                upper = kind >= SUB
                index = kind & (SUB - 1)
                depth = depth + pick(tables[0], tables[1], index, upper) * (rho / (1.0 + rho))
                after = jnp.exp2(-depth)
                weight = (through - after) * shade
                through = after
                for channel in range(3):
                    sums[channel] = sums[channel] + weight * pick(
                        tables[2 + 2 * channel], tables[3 + 2 * channel], index, upper
                    )
            red, green, blue = (quantize(jnp.log2(value), LOG_LOW, LOG_STEP) for value in sums)
            deep = quantize(depth, 0.0, TAU_STEP)
            spot = base * stride + step * PER + c
            out_ref[pl.ds(spot, SUB, stride=stride), :] = (red << 16) | green
            out_ref[pl.ds(spot + blocks, SUB, stride=stride), :] = (blue << 16) | deep
        return carry

    lax.fori_loop(0, rows // SUB, row_block, 0)


def shade_bricks(density, low, high, material, tables, band):
    ghost, rows, columns = density.shape
    slices = material.shape[0]
    steps = columns // CB
    blocks = columns // LANES
    return pl.pallas_call(
        functools.partial(shade_kernel, blocks),
        grid=(steps,),
        in_specs=[
            pl.BlockSpec((ghost, rows, LANES), lambda i: (0, 0, jnp.maximum(PER * i - 1, 0))),
            pl.BlockSpec((ghost, rows, CB), lambda i: (0, 0, i)),
            pl.BlockSpec((ghost, rows, LANES), lambda i: (0, 0, jnp.minimum(PER * i + PER, blocks - 1))),
            pl.BlockSpec((ghost, 1, CB), lambda i: (0, 0, i)),
            pl.BlockSpec((ghost, 1, CB), lambda i: (0, 0, i)),
            pl.BlockSpec((slices, rows, CB), lambda i: (0, 0, i)),
            pl.BlockSpec((8, SUB, LANES), lambda i: (0, 0, 0)),
            pl.BlockSpec(
                (1, CB + 2 * LANES, CB),
                lambda i: (jnp.where(i == 0, 0, jnp.where(i == steps - 1, 2, 1)), 0, 0),
            ),
        ],
        out_specs=pl.BlockSpec((rows * 2 * blocks, LANES), lambda i: (0, 0)),
        out_shape=jax.ShapeDtypeStruct((rows * 2 * blocks, LANES), jnp.int32),
        scratch_shapes=[
            pltpu.VMEM((ghost, PER, rows + 2 * SUB, LANES), jnp.float32),
            pltpu.VMEM((slices, rows, CB), jnp.float32),
        ],
        compiler_params=pltpu.CompilerParams(vmem_limit_bytes=56 << 20),
    )(density, density, density, low, high, material, tables, band)


def blend_kernel(order_ref, part_ref, out_ref, place, image):
    bricks, rows, pairs, blocks, lanes = part_ref.shape
    for brick in range(bricks):
        place[order_ref[brick]] = brick
    for row in range(rows):
        for group in range(blocks // SUB):
            spots = pl.ds(group * SUB, SUB)

            def walk(rank, carry, row=row, spots=spots):
                front, red, green, blue = carry
                brick = place[rank]
                first = part_ref[brick, row, 0, spots, :]
                second = part_ref[brick, row, 1, spots, :]

                def seen(code):
                    return jnp.exp2(code.astype(jnp.float32) * LOG_STEP + (LOG_LOW - front))

                red = red + seen(lax.shift_right_logical(first, 16))
                green = green + seen(first & 0xFFFF)
                blue = blue + seen(lax.shift_right_logical(second, 16))
                front = front + (second & 0xFFFF).astype(jnp.float32) * TAU_STEP
                return front, red, green, blue

            zero = jnp.zeros((SUB, lanes), jnp.float32)
            front, red, green, blue = lax.fori_loop(0, bricks, walk, (zero,) * 4, unroll=4)
            for channel, value in enumerate((red, green, blue, 1.0 - jnp.exp2(-front))):
                image[pl.ds((row * 4 + channel) * blocks + group * SUB, SUB), :] = value
        for block in range(blocks):
            out_ref[row, :, pl.ds(block * lanes, lanes)] = image[pl.ds(row * 4 * blocks + block, 4, stride=blocks), :]


def blend(order, part):
    bricks, rows, pairs, blocks, lanes = part.shape
    return pl.pallas_call(
        blend_kernel,
        in_specs=[pl.BlockSpec(memory_space=pltpu.SMEM), pl.BlockSpec(memory_space=pltpu.VMEM)],
        out_specs=pl.BlockSpec(memory_space=pltpu.VMEM),
        out_shape=jax.ShapeDtypeStruct((rows, 4, blocks * lanes), jnp.float32),
        scratch_shapes=[pltpu.SMEM((bricks,), jnp.int32), pltpu.VMEM((rows * 4 * blocks, lanes), jnp.float32)],
    )(order, part)


def band_matrices():
    source = jnp.arange(CB + 2 * LANES)[:, None] - LANES
    target = jnp.arange(CB)[None, :]
    inner = (source == target + 1).astype(jnp.float32) - (source == target - 1).astype(jnp.float32)
    first = jnp.where(source < 0, 0.0, inner)
    last = jnp.where(source >= CB, 0.0, inner)
    return jnp.stack([first, inner, last]).astype(jnp.bfloat16)


def body(density, material, order, color_table, extinction):
    count = lax.axis_size("screen")
    rows, columns = density.shape[1], density.shape[2]
    bricks = lax.axis_size("depth")
    forward = [(i, i + 1) for i in range(count - 1)]
    backward = [(target, source) for source, target in forward]
    low = lax.ppermute(density[:, rows - 1 :], "screen", forward)
    high = lax.ppermute(density[:, :1], "screen", backward)
    entries = jnp.concatenate([(LOG2E * extinction)[None], color_table.T], axis=0)
    tables = jnp.broadcast_to(entries.reshape(8, SUB, 1), (8, SUB, LANES))
    coded = shade_bricks(density, low, high, material, tables, band_matrices())
    blocks = columns // LANES
    strip = rows // bricks
    parts = coded.reshape(bricks, strip * 2 * blocks, LANES)
    parts = lax.all_to_all(parts, "depth", split_axis=0, concat_axis=0, tiled=True)
    image = blend(order, parts.reshape(bricks, strip, 2, blocks, LANES))
    return image.transpose(1, 0, 2)


def solution(mesh):
    placed = (P("depth", "screen", None), P("depth", "screen", None), P(), P(), P())
    return jax.shard_map(
        body,
        mesh=mesh,
        in_specs=placed,
        out_specs=P(None, ("screen", "depth"), None),
        check_vma=False,
    )
```

```python
import functools
import math

import jax
import jax.numpy as jnp
from jax import lax
from jax.experimental import pallas as pl
from jax.experimental.pallas import tpu as pltpu
from jax.sharding import PartitionSpec as P

light_x = 0.48
light_y = 0.6
light_z = 0.64
ambient = 0.55
diffuse = 0.45

LANES = 128
SUB = 8
CB = 256
PER = CB // LANES
CHUNK = 32
LANE_TABLES = 1
LOG2E = math.log2(math.e)

SLICES = 8
TAU_TOP = SLICES * 0.0390625 * (10.0 / 11.0) * LOG2E * 1.001
LOG_TOP = 0.0
LOG_LOW = -14.0
LEVELS = 65535.0
TAU_STEP = TAU_TOP / LEVELS
LOG_STEP = (LOG_TOP - LOG_LOW) / LEVELS


def quantize(value, low, step):
    return (value * (1.0 / step) + (0.5 - low / step)).astype(jnp.int32)


def entries_at(table, index):
    numbers = lax.GatherDimensionNumbers(
        offset_dims=(),
        collapsed_slice_dims=(0,),
        start_index_map=(0,),
        operand_batching_dims=(1,),
        start_indices_batching_dims=(1,),
    )
    return lax.gather(
        table, index[..., None], numbers, (1, 1), mode=lax.GatherScatterMode.PROMISE_IN_BOUNDS
    )


def lane_entries(table, index):
    numbers = lax.GatherDimensionNumbers(
        offset_dims=(),
        collapsed_slice_dims=(1,),
        start_index_map=(1,),
        operand_batching_dims=(0,),
        start_indices_batching_dims=(0,),
    )
    return lax.gather(
        table, index[..., None], numbers, (1, 1), mode=lax.GatherScatterMode.PROMISE_IN_BOUNDS
    )


def pick(low_table, high_table, index, upper):
    return jnp.where(upper, entries_at(high_table, index), entries_at(low_table, index))


def shade_kernel(den_hbm, low_ref, high_ref, mat_hbm, color_hbm, ext_hbm, out_ref, den, mat, full, diff, table, band, color_ref, ext_ref, den_sem, mat_sem, table_sem):
    ghost, rows, columns = den.shape
    slices = ghost - 2
    steps = columns // CB
    blocks = columns // LANES
    stride = 2 * blocks

    def den_copy(j):
        cols = pl.ds(pl.multiple_of(j * CB, CB), CB)
        return pltpu.make_async_copy(den_hbm.at[:, :, cols], den.at[:, :, cols], den_sem.at[j])

    def mat_copy(j):
        cols = pl.ds(pl.multiple_of(j * CB, CB), CB)
        return pltpu.make_async_copy(mat_hbm.at[:, :, cols], mat.at[:, :, cols], mat_sem.at[j])

    color_copy = pltpu.make_async_copy(color_hbm, color_ref, table_sem.at[0])
    ext_copy = pltpu.make_async_copy(ext_hbm, ext_ref, table_sem.at[1])
    color_copy.start()
    ext_copy.start()
    den_copy(0).start()
    den_copy(1).start()
    for j in range(steps):
        mat_copy(j).start()
        if j + 2 < steps:
            den_copy(j + 2).start()

    source = lax.broadcasted_iota(jnp.int32, (2 * SUB, LANES), 0)
    target = lax.broadcasted_iota(jnp.int32, (2 * SUB, LANES), 1)
    for top in range(0, CB + 2 * LANES, 2 * SUB):
        for side in range(0, CB, LANES):
            shift = (source + (top - LANES)) - (target + side)
            tile = (shift == 1).astype(jnp.float32) - (shift == -1).astype(jnp.float32)
            band[top : top + 2 * SUB, side : side + LANES] = tile.astype(jnp.bfloat16)
    color_copy.wait()
    ext_copy.wait()
    lane = lax.broadcasted_iota(jnp.int32, (SUB, LANES), 1)
    for channel in range(LANE_TABLES):
        spread = jnp.zeros((SUB, LANES), jnp.float32)
        for entry in range(2 * SUB):
            spread = jnp.where(lane == entry, (diffuse * light_x) * color_ref[channel, entry], spread)
        table[2 + 2 * channel] = spread
    for entry in range(SUB):
        for half in range(2):
            spot = entry + half * SUB
            table[half, entry : entry + 1, :] = jnp.full((1, LANES), -LOG2E * ext_ref[spot], jnp.float32)
            for channel in range(LANE_TABLES, 3):
                scale = (diffuse * light_x) * color_ref[channel, spot]
                table[2 + 2 * channel + half, entry : entry + 1, :] = jnp.full((1, LANES), scale, jnp.float32)
    tables = [table[i] for i in range(8)]

    def shade_columns(j, carry):
        @pl.when(j + 1 < steps)
        def _():
            den_copy(j + 1).wait()

        mat_copy(j).wait()
        start = pl.multiple_of(j * CB, CB)
        left = pl.multiple_of(jnp.maximum(start - LANES, 0), LANES)
        right = pl.multiple_of(jnp.minimum(start + CB, columns - LANES), LANES)
        inside_left = jnp.where(j == 0, 0.0, 1.0).astype(jnp.bfloat16)
        inside_right = jnp.where(j == steps - 1, 0.0, 1.0).astype(jnp.bfloat16)

        def fill(r):
            for z in range(ghost):
                for c in range(PER):
                    cols = pl.ds(start + c * LANES, LANES)
                    if r == 0:
                        full[z, c, SUB - 1 : SUB, :] = low_ref[z, :, cols].astype(jnp.float32)
                    full[z, c, pl.ds(SUB + r * CHUNK, CHUNK), :] = den[z, pl.ds(r * CHUNK, CHUNK), cols].astype(jnp.float32)
                    if r == rows // CHUNK - 1:
                        full[z, c, SUB + rows : SUB + rows + 1, :] = high_ref[z, :, cols].astype(jnp.float32)

        def across(r):
            spots = pl.ds(r * CHUNK, CHUNK)
            window = jnp.concatenate(
                [
                    den[1:-1, spots, pl.ds(left, LANES)] * inside_left,
                    den[1:-1, spots, pl.ds(start, CB)],
                    den[1:-1, spots, pl.ds(right, LANES)] * inside_right,
                ],
                axis=-1,
            )
            diff[:, spots, :] = jnp.dot(
                window.reshape(slices * CHUNK, CB + 2 * LANES), band[...], preferred_element_type=jnp.float32
            ).reshape(slices, CHUNK, CB)

        def shade_tile(base, c):
            spots = pl.ds(base, SUB)
            through = jnp.ones((SUB, LANES), jnp.float32)
            depth = jnp.zeros((SUB, LANES), jnp.float32)
            sums = [jnp.zeros((SUB, LANES), jnp.float32) for _ in range(3)]
            for z in range(slices):
                rho = full[z + 1, c, pl.ds(base + SUB, SUB), :]
                dz = full[z + 2, c, pl.ds(base + SUB, SUB), :] - full[z, c, pl.ds(base + SUB, SUB), :]
                dy = full[z + 1, c, pl.ds(base + SUB + 1, SUB), :] - full[z + 1, c, pl.ds(base + SUB - 1, SUB), :]
                dx = diff[z, spots, pl.ds(c * LANES, LANES)]
                lit = dx + (light_y / light_x) * dy + (light_z / light_x) * dz
                bend = lax.rsqrt(4.0 + dx * dx + dy * dy + dz * dz)
                shade = ambient / (diffuse * light_x) + lit * bend
                kind = mat[z, spots, pl.ds(start + c * LANES, LANES)]
                upper = kind >= SUB
                index = kind & (SUB - 1)
                depth = depth + pick(tables[0], tables[1], index, upper) * (rho * (1.0 / (1.0 + rho)))
                after = jnp.exp2(depth)
                weight = (through - after) * shade
                through = after
                for channel in range(3):
                    if channel < LANE_TABLES:
                        color = lane_entries(tables[2 + 2 * channel], kind)
                    else:
                        color = pick(tables[2 + 2 * channel], tables[3 + 2 * channel], index, upper)
                    sums[channel] = sums[channel] + weight * color
            red, green, blue = (quantize(jnp.log2(value), LOG_LOW, LOG_STEP) for value in sums)
            deep = quantize(depth, 0.0, -TAU_STEP)
            spot = base * stride + j * PER + c
            out_ref[pl.ds(spot, SUB, stride=stride), :] = (red << 16) | green
            out_ref[pl.ds(spot + blocks, SUB, stride=stride), :] = (blue << 16) | deep

        chunks = rows // CHUNK
        fill(0)
        across(0)
        for r in range(chunks):
            if r + 1 < chunks:
                fill(r + 1)
                across(r + 1)
            for base in range(r * CHUNK, (r + 1) * CHUNK, SUB):
                for c in range(PER):
                    shade_tile(base, c)
        return carry

    den_copy(0).wait()
    lax.fori_loop(0, steps, shade_columns, 0)


def shade_bricks(density, low, high, material, color_table, extinction):
    ghost, rows, columns = density.shape
    slices = material.shape[0]
    steps = columns // CB
    blocks = columns // LANES
    return pl.pallas_call(
        shade_kernel,
        in_specs=[
            pl.BlockSpec(memory_space=pltpu.HBM),
            pl.BlockSpec(memory_space=pltpu.VMEM),
            pl.BlockSpec(memory_space=pltpu.VMEM),
            pl.BlockSpec(memory_space=pltpu.HBM),
            pl.BlockSpec(memory_space=pltpu.HBM),
            pl.BlockSpec(memory_space=pltpu.HBM),
        ],
        out_specs=pl.BlockSpec(memory_space=pltpu.VMEM),
        out_shape=jax.ShapeDtypeStruct((rows * 2 * blocks, LANES), jnp.int32),
        scratch_shapes=[
            pltpu.VMEM((ghost, rows, columns), jnp.bfloat16),
            pltpu.VMEM((slices, rows, columns), jnp.int32),
            pltpu.VMEM((ghost, PER, rows + 2 * SUB, LANES), jnp.float32),
            pltpu.VMEM((slices, rows, CB), jnp.float32),
            pltpu.VMEM((8, SUB, LANES), jnp.float32),
            pltpu.VMEM((CB + 2 * LANES, CB), jnp.bfloat16),
            pltpu.SMEM(color_table.shape, jnp.float32),
            pltpu.SMEM(extinction.shape, jnp.float32),
            pltpu.SemaphoreType.DMA((steps,)),
            pltpu.SemaphoreType.DMA((steps,)),
            pltpu.SemaphoreType.DMA((2,)),
        ],
        compiler_params=pltpu.CompilerParams(vmem_limit_bytes=61 << 20),
    )(density, low, high, material, color_table, extinction)


def blend_kernel(order_ref, part_ref, out_ref, place, image):
    bricks, rows, pairs, blocks, lanes = part_ref.shape
    for brick in range(bricks):
        place[order_ref[brick]] = brick
    spots = [(row, group) for row in range(rows) for group in range(0, blocks, SUB)]

    def walk(rank, carry):
        brick = place[rank]
        after = []
        for (row, group), (front, red, green, blue) in zip(spots, carry):
            first = part_ref[brick, row, 0, group : group + SUB, :]
            second = part_ref[brick, row, 1, group : group + SUB, :]
            low = LOG_LOW - front

            def seen(code):
                return jnp.exp2(code.astype(jnp.float32) * LOG_STEP + low)

            red = red + seen(lax.shift_right_logical(first, 16))
            green = green + seen(first & 0xFFFF)
            blue = blue + seen(lax.shift_right_logical(second, 16))
            front = front + (second & 0xFFFF).astype(jnp.float32) * TAU_STEP
            after.append((front, red, green, blue))
        return tuple(after)

    zero = jnp.zeros((SUB, lanes), jnp.float32)
    sums = lax.fori_loop(0, bricks, walk, tuple((zero,) * 4 for _ in spots), unroll=2)
    for (row, group), (front, red, green, blue) in zip(spots, sums):
        for channel, value in enumerate((red, green, blue, 1.0 - jnp.exp2(-front))):
            image[pl.ds((row * 4 + channel) * blocks + group, SUB), :] = value
    for row in range(rows):
        for block in range(blocks):
            out_ref[row, :, pl.ds(block * lanes, lanes)] = image[pl.ds(row * 4 * blocks + block, 4, stride=blocks), :]


def blend(order, part):
    bricks, rows, pairs, blocks, lanes = part.shape
    return pl.pallas_call(
        blend_kernel,
        in_specs=[pl.BlockSpec(memory_space=pltpu.SMEM), pl.BlockSpec(memory_space=pltpu.VMEM)],
        out_specs=pl.BlockSpec(memory_space=pltpu.VMEM),
        out_shape=jax.ShapeDtypeStruct((rows, 4, blocks * lanes), jnp.float32),
        scratch_shapes=[pltpu.SMEM((bricks,), jnp.int32), pltpu.VMEM((rows * 4 * blocks, lanes), jnp.float32)],
        compiler_params=pltpu.CompilerParams(vmem_limit_bytes=8 << 20),
    )(order, part)


def body(density, material, order, color_table, extinction):
    count = lax.axis_size("screen")
    rows, columns = density.shape[1], density.shape[2]
    bricks = lax.axis_size("depth")
    forward = [(i, i + 1) for i in range(count - 1)]
    backward = [(target, source) for source, target in forward]
    low = lax.ppermute(density[:, rows - 1 :], "screen", forward)
    high = lax.ppermute(density[:, :1], "screen", backward)
    coded = shade_bricks(density, low, high, material, color_table.T, extinction)
    blocks = columns // LANES
    strip = rows // bricks
    parts = coded.reshape(bricks, strip * 2 * blocks, LANES)
    parts = lax.all_to_all(parts, "depth", split_axis=0, concat_axis=0, tiled=True)
    image = blend(order, parts.reshape(bricks, strip, 2, blocks, LANES))
    return image.transpose(1, 0, 2)


def solution(mesh):
    placed = (P("depth", "screen", None), P("depth", "screen", None), P(), P(), P())
    return jax.shard_map(
        body,
        mesh=mesh,
        in_specs=placed,
        out_specs=P(None, ("screen", "depth"), None),
        check_vma=False,
    )
```

```python
import functools
import math

import jax
import jax.numpy as jnp
from jax import lax
from jax.experimental import pallas as pl
from jax.experimental.pallas import tpu as pltpu
from jax.sharding import PartitionSpec as P

light_x = 0.48
light_y = 0.6
light_z = 0.64
ambient = 0.55
diffuse = 0.45

LANES = 128
SUB = 8
CB = 256
PER = CB // LANES
CHUNK = 32
VLIM = 52
LANE_TABLES = 2
LOG2E = math.log2(math.e)

SLICES = 8
TAU_TOP = SLICES * 0.0390625 * (10.0 / 11.0) * LOG2E * 1.001
LOG_TOP = 0.0
LOG_LOW = -14.0
LEVELS = 65535.0
TAU_STEP = TAU_TOP / LEVELS
LOG_STEP = (LOG_TOP - LOG_LOW) / LEVELS


def quantize(value, low, step):
    return (value * (1.0 / step) + (0.5 - low / step)).astype(jnp.int32)


def entries_at(table, index):
    numbers = lax.GatherDimensionNumbers(
        offset_dims=(),
        collapsed_slice_dims=(0,),
        start_index_map=(0,),
        operand_batching_dims=(1,),
        start_indices_batching_dims=(1,),
    )
    return lax.gather(
        table, index[..., None], numbers, (1, 1), mode=lax.GatherScatterMode.PROMISE_IN_BOUNDS
    )


def lane_entries(table, index):
    numbers = lax.GatherDimensionNumbers(
        offset_dims=(),
        collapsed_slice_dims=(1,),
        start_index_map=(1,),
        operand_batching_dims=(0,),
        start_indices_batching_dims=(0,),
    )
    return lax.gather(
        table, index[..., None], numbers, (1, 1), mode=lax.GatherScatterMode.PROMISE_IN_BOUNDS
    )


def pick(low_table, high_table, index, upper):
    return jnp.where(upper, entries_at(high_table, index), entries_at(low_table, index))


def shade_kernel(den_hbm, low_ref, high_ref, mat_hbm, color_hbm, ext_hbm, out_ref, den, mat, full, diff, table, band, color_ref, ext_ref, den_sem, mat_sem, table_sem):
    ghost, rows, columns = den.shape
    slices = ghost - 2
    steps = columns // CB
    blocks = columns // LANES
    stride = 2 * blocks

    def den_copy(j):
        cols = pl.ds(pl.multiple_of(j * CB, CB), CB)
        return pltpu.make_async_copy(den_hbm.at[:, :, cols], den.at[:, :, cols], den_sem.at[j])

    def mat_copy(j):
        cols = pl.ds(pl.multiple_of(j * CB, CB), CB)
        return pltpu.make_async_copy(mat_hbm.at[:, :, cols], mat.at[:, :, cols], mat_sem.at[j])

    color_copy = pltpu.make_async_copy(color_hbm, color_ref, table_sem.at[0])
    ext_copy = pltpu.make_async_copy(ext_hbm, ext_ref, table_sem.at[1])
    color_copy.start()
    ext_copy.start()
    den_copy(0).start()
    mat_copy(0).start()
    den_copy(1).start()
    mat_copy(1).start()

    source = lax.broadcasted_iota(jnp.int32, (2 * SUB, LANES), 0)
    target = lax.broadcasted_iota(jnp.int32, (2 * SUB, LANES), 1)
    for top in range(0, CB + 2 * LANES, 2 * SUB):
        for side in range(0, CB, LANES):
            shift = (source + (top - LANES)) - (target + side)
            tile = (shift == 1).astype(jnp.float32) - (shift == -1).astype(jnp.float32)
            band[top : top + 2 * SUB, side : side + LANES] = tile.astype(jnp.bfloat16)
    color_copy.wait()
    ext_copy.wait()
    lane = lax.broadcasted_iota(jnp.int32, (SUB, LANES), 1)
    for channel in range(LANE_TABLES):
        spread = jnp.zeros((SUB, LANES), jnp.float32)
        for entry in range(2 * SUB):
            spread = jnp.where(lane == entry, color_ref[channel, entry], spread)
        table[2 + 2 * channel] = spread
    for entry in range(SUB):
        for half in range(2):
            spot = entry + half * SUB
            table[half, entry : entry + 1, :] = jnp.full((1, LANES), ext_ref[spot], jnp.float32)
            for channel in range(LANE_TABLES, 3):
                scale = color_ref[channel, spot]
                table[2 + 2 * channel + half, entry : entry + 1, :] = jnp.full((1, LANES), scale, jnp.float32)
    tables = [table[i] for i in range(8)]

    def shade_columns(j, carry):
        @pl.when(j + 1 < steps)
        def _():
            den_copy(j + 1).wait()

        mat_copy(j).wait()

        @pl.when(j + 2 < steps)
        def _():
            den_copy(j + 2).start()
            mat_copy(j + 2).start()

        start = pl.multiple_of(j * CB, CB)
        left = pl.multiple_of(jnp.maximum(start - LANES, 0), LANES)
        right = pl.multiple_of(jnp.minimum(start + CB, columns - LANES), LANES)
        inside_left = jnp.where(j == 0, 0.0, 1.0).astype(jnp.bfloat16)
        inside_right = jnp.where(j == steps - 1, 0.0, 1.0).astype(jnp.bfloat16)

        def fill(r):
            for z in range(ghost):
                for c in range(PER):
                    cols = pl.ds(start + c * LANES, LANES)
                    if r == 0:
                        full[z, c, SUB - 1 : SUB, :] = low_ref[z, :, cols].astype(jnp.float32)
                    full[z, c, pl.ds(SUB + r * CHUNK, CHUNK), :] = den[z, pl.ds(r * CHUNK, CHUNK), cols].astype(jnp.float32)
                    if r == rows // CHUNK - 1:
                        full[z, c, SUB + rows : SUB + rows + 1, :] = high_ref[z, :, cols].astype(jnp.float32)

        def across(r):
            spots = pl.ds(r * CHUNK, CHUNK)
            window = jnp.concatenate(
                [
                    den[1:-1, spots, pl.ds(left, LANES)] * inside_left,
                    den[1:-1, spots, pl.ds(start, CB)],
                    den[1:-1, spots, pl.ds(right, LANES)] * inside_right,
                ],
                axis=-1,
            )
            diff[:, spots, :] = jnp.dot(
                window.reshape(slices * CHUNK, CB + 2 * LANES), band[...], preferred_element_type=jnp.float32
            ).reshape(slices, CHUNK, CB)

        def shade_tile(base, c):
            spots = pl.ds(base, SUB)
            through = jnp.ones((SUB, LANES), jnp.float32)
            depth = jnp.zeros((SUB, LANES), jnp.float32)
            sums = [jnp.zeros((SUB, LANES), jnp.float32) for _ in range(3)]
            for z in range(slices):
                rho = full[z + 1, c, pl.ds(base + SUB, SUB), :]
                dz = full[z + 2, c, pl.ds(base + SUB, SUB), :] - full[z, c, pl.ds(base + SUB, SUB), :]
                dy = full[z + 1, c, pl.ds(base + SUB + 1, SUB), :] - full[z + 1, c, pl.ds(base + SUB - 1, SUB), :]
                dx = diff[z, spots, pl.ds(c * LANES, LANES)]
                lit = dx + (light_y / light_x) * dy + (light_z / light_x) * dz
                bend = lax.rsqrt(4.0 + dx * dx + dy * dy + dz * dz)
                shade = ambient / (diffuse * light_x) + lit * bend
                kind = mat[z, spots, pl.ds(start + c * LANES, LANES)]
                upper = kind >= SUB
                index = kind & (SUB - 1)
                depth = depth + pick(tables[0], tables[1], index, upper) * (rho * (1.0 / (1.0 + rho)))
                after = jnp.exp2(depth)
                weight = (through - after) * shade
                through = after
                for channel in range(3):
                    if channel < LANE_TABLES:
                        color = lane_entries(tables[2 + 2 * channel], kind)
                    else:
                        color = pick(tables[2 + 2 * channel], tables[3 + 2 * channel], index, upper)
                    sums[channel] = sums[channel] + weight * color
            red, green, blue = (quantize(jnp.log2(value), LOG_LOW, LOG_STEP) for value in sums)
            deep = quantize(depth, 0.0, -TAU_STEP)
            spot = base * stride + j * PER + c
            out_ref[pl.ds(spot, SUB, stride=stride), :] = (red << 16) | green
            out_ref[pl.ds(spot + blocks, SUB, stride=stride), :] = (blue << 16) | deep

        chunks = rows // CHUNK
        fill(0)
        across(0)
        for r in range(chunks):
            if r + 1 < chunks:
                fill(r + 1)
                across(r + 1)
            for base in range(r * CHUNK, (r + 1) * CHUNK, SUB):
                for c in range(PER):
                    shade_tile(base, c)
        return carry

    den_copy(0).wait()
    lax.fori_loop(0, steps, shade_columns, 0)


def shade_bricks(density, low, high, material, color_table, extinction):
    ghost, rows, columns = density.shape
    slices = material.shape[0]
    steps = columns // CB
    blocks = columns // LANES
    return pl.pallas_call(
        shade_kernel,
        in_specs=[
            pl.BlockSpec(memory_space=pltpu.HBM),
            pl.BlockSpec(memory_space=pltpu.VMEM),
            pl.BlockSpec(memory_space=pltpu.VMEM),
            pl.BlockSpec(memory_space=pltpu.HBM),
            pl.BlockSpec(memory_space=pltpu.HBM),
            pl.BlockSpec(memory_space=pltpu.HBM),
        ],
        out_specs=pl.BlockSpec(memory_space=pltpu.VMEM),
        out_shape=jax.ShapeDtypeStruct((rows * 2 * blocks, LANES), jnp.int32),
        scratch_shapes=[
            pltpu.VMEM((ghost, rows, columns), jnp.bfloat16),
            pltpu.VMEM((slices, rows, columns), jnp.int32),
            pltpu.VMEM((ghost, PER, rows + 2 * SUB, LANES), jnp.float32),
            pltpu.VMEM((slices, rows, CB), jnp.float32),
            pltpu.VMEM((8, SUB, LANES), jnp.float32),
            pltpu.VMEM((CB + 2 * LANES, CB), jnp.bfloat16),
            pltpu.SMEM(color_table.shape, jnp.float32),
            pltpu.SMEM(extinction.shape, jnp.float32),
            pltpu.SemaphoreType.DMA((steps,)),
            pltpu.SemaphoreType.DMA((steps,)),
            pltpu.SemaphoreType.DMA((2,)),
        ],
        compiler_params=pltpu.CompilerParams(vmem_limit_bytes=VLIM << 20),
    )(density, low, high, material, (diffuse * light_x) * color_table, -LOG2E * extinction)


def blend_kernel(order_ref, part_ref, out_ref, place, image):
    bricks, rows, pairs, blocks, lanes = part_ref.shape
    for brick in range(bricks):
        place[order_ref[brick]] = brick
    spots = [(row, group) for row in range(rows) for group in range(0, blocks, SUB)]

    def walk(rank, carry):
        brick = place[rank]
        after = []
        for (row, group), (front, red, green, blue) in zip(spots, carry):
            first = part_ref[brick, row, 0, group : group + SUB, :]
            second = part_ref[brick, row, 1, group : group + SUB, :]
            low = LOG_LOW - front

            def seen(code):
                return jnp.exp2(code.astype(jnp.float32) * LOG_STEP + low)

            red = red + seen(lax.shift_right_logical(first, 16))
            green = green + seen(first & 0xFFFF)
            blue = blue + seen(lax.shift_right_logical(second, 16))
            front = front + (second & 0xFFFF).astype(jnp.float32) * TAU_STEP
            after.append((front, red, green, blue))
        return tuple(after)

    zero = jnp.zeros((SUB, lanes), jnp.float32)
    sums = lax.fori_loop(0, bricks, walk, tuple((zero,) * 4 for _ in spots), unroll=4)
    for (row, group), (front, red, green, blue) in zip(spots, sums):
        for channel, value in enumerate((red, green, blue, 1.0 - jnp.exp2(-front))):
            image[pl.ds((row * 4 + channel) * blocks + group, SUB), :] = value
    for row in range(rows):
        for block in range(blocks):
            out_ref[row, :, pl.ds(block * lanes, lanes)] = image[pl.ds(row * 4 * blocks + block, 4, stride=blocks), :]


def blend(order, part):
    bricks, rows, pairs, blocks, lanes = part.shape
    return pl.pallas_call(
        blend_kernel,
        in_specs=[pl.BlockSpec(memory_space=pltpu.SMEM), pl.BlockSpec(memory_space=pltpu.VMEM)],
        out_specs=pl.BlockSpec(memory_space=pltpu.VMEM),
        out_shape=jax.ShapeDtypeStruct((rows, 4, blocks * lanes), jnp.float32),
        scratch_shapes=[pltpu.SMEM((bricks,), jnp.int32), pltpu.VMEM((rows * 4 * blocks, lanes), jnp.float32)],
        compiler_params=pltpu.CompilerParams(vmem_limit_bytes=8 << 20),
    )(order, part)


def body(density, material, order, color_table, extinction):
    count = lax.axis_size("screen")
    rows, columns = density.shape[1], density.shape[2]
    bricks = lax.axis_size("depth")
    forward = [(i, i + 1) for i in range(count - 1)]
    backward = [(target, source) for source, target in forward]
    low = lax.ppermute(density[:, rows - 1 :], "screen", forward)
    high = lax.ppermute(density[:, :1], "screen", backward)
    coded = shade_bricks(density, low, high, material, color_table.T, extinction)
    blocks = columns // LANES
    strip = rows // bricks
    parts = coded.reshape(bricks, strip * 2 * blocks, LANES)
    parts = lax.all_to_all(parts, "depth", split_axis=0, concat_axis=0, tiled=True)
    image = blend(order, parts.reshape(bricks, strip, 2, blocks, LANES))
    return image.transpose(1, 0, 2)


def solution(mesh):
    placed = (P("depth", "screen", None), P("depth", "screen", None), P(), P(), P())
    return jax.shard_map(
        body,
        mesh=mesh,
        in_specs=placed,
        out_specs=P(None, ("screen", "depth"), None),
        check_vma=False,
    )
```

```python
import functools
import math

import jax
import jax.numpy as jnp
from jax import lax
from jax.experimental import pallas as pl
from jax.experimental.pallas import tpu as pltpu
from jax.sharding import PartitionSpec as P

light_x = 0.48
light_y = 0.6
light_z = 0.64
ambient = 0.55
diffuse = 0.45

LANES = 128
SUB = 8
CB = 256
PER = CB // LANES
CHUNK = 32
VLIM = 52
LANE_TABLES = 2
LOG2E = math.log2(math.e)

SLICES = 8
TAU_TOP = SLICES * 0.0390625 * (10.0 / 11.0) * LOG2E * 1.001
LOG_TOP = 0.0
LOG_LOW = -14.0
LEVELS = 65535.0
TAU_STEP = TAU_TOP / LEVELS
LOG_STEP = (LOG_TOP - LOG_LOW) / LEVELS


def quantize(value, low, step):
    return (value * (1.0 / step) + (0.5 - low / step)).astype(jnp.int32)


def entries_at(table, index):
    numbers = lax.GatherDimensionNumbers(
        offset_dims=(),
        collapsed_slice_dims=(0,),
        start_index_map=(0,),
        operand_batching_dims=(1,),
        start_indices_batching_dims=(1,),
    )
    return lax.gather(
        table, index[..., None], numbers, (1, 1), mode=lax.GatherScatterMode.PROMISE_IN_BOUNDS
    )


def lane_entries(table, index):
    numbers = lax.GatherDimensionNumbers(
        offset_dims=(),
        collapsed_slice_dims=(1,),
        start_index_map=(1,),
        operand_batching_dims=(0,),
        start_indices_batching_dims=(0,),
    )
    return lax.gather(
        table, index[..., None], numbers, (1, 1), mode=lax.GatherScatterMode.PROMISE_IN_BOUNDS
    )


def pick(low_table, high_table, index, upper):
    return jnp.where(upper, entries_at(high_table, index), entries_at(low_table, index))


def prepare_kernel(color_ref, ext_ref, table, band):
    source = lax.broadcasted_iota(jnp.int32, (2 * SUB, LANES), 0)
    target = lax.broadcasted_iota(jnp.int32, (2 * SUB, LANES), 1)
    for top in range(0, CB + 2 * LANES, 2 * SUB):
        for side in range(0, CB, LANES):
            shift = (source + (top - LANES)) - (target + side)
            tile = (shift == 1).astype(jnp.float32) - (shift == -1).astype(jnp.float32)
            band[top : top + 2 * SUB, side : side + LANES] = tile.astype(jnp.bfloat16)
    lane = lax.broadcasted_iota(jnp.int32, (SUB, LANES), 1)
    for channel in range(LANE_TABLES):
        table[3 + 2 * channel] = jnp.zeros((SUB, LANES), jnp.float32)
        spread = jnp.zeros((SUB, LANES), jnp.float32)
        for entry in range(2 * SUB):
            spread = jnp.where(lane == entry, (diffuse * light_x) * color_ref[channel, entry], spread)
        table[2 + 2 * channel] = spread
    for entry in range(SUB):
        for half in range(2):
            spot = entry + half * SUB
            table[half, entry : entry + 1, :] = jnp.full((1, LANES), -LOG2E * ext_ref[spot], jnp.float32)
            for channel in range(LANE_TABLES, 3):
                scale = (diffuse * light_x) * color_ref[channel, spot]
                table[2 + 2 * channel + half, entry : entry + 1, :] = jnp.full((1, LANES), scale, jnp.float32)


def prepare(color_table, extinction):
    smem = pl.BlockSpec(memory_space=pltpu.SMEM)
    vmem = pl.BlockSpec(memory_space=pltpu.VMEM)
    return pl.pallas_call(
        prepare_kernel,
        in_specs=[smem, smem],
        out_specs=[vmem, vmem],
        out_shape=[
            jax.ShapeDtypeStruct((8, SUB, LANES), jnp.float32),
            jax.ShapeDtypeStruct((CB + 2 * LANES, CB), jnp.bfloat16),
        ],
        compiler_params=pltpu.CompilerParams(vmem_limit_bytes=VLIM << 20),
    )(color_table, extinction)


def shade_kernel(den_hbm, low_ref, high_ref, mat_hbm, table, band, out_ref, den, mat, full, diff, den_sem, mat_sem):
    ghost, rows, columns = den.shape
    slices = ghost - 2
    steps = columns // CB
    blocks = columns // LANES
    stride = 2 * blocks

    def den_copy(j):
        cols = pl.ds(pl.multiple_of(j * CB, CB), CB)
        return pltpu.make_async_copy(den_hbm.at[:, :, cols], den.at[:, :, cols], den_sem.at[j])

    def mat_copy(j):
        cols = pl.ds(pl.multiple_of(j * CB, CB), CB)
        return pltpu.make_async_copy(mat_hbm.at[:, :, cols], mat.at[:, :, cols], mat_sem.at[j])

    den_copy(0).start()
    mat_copy(0).start()
    den_copy(1).start()
    mat_copy(1).start()

    tables = [table[i] for i in range(8)]

    def shade_columns(j, carry):
        @pl.when(j + 1 < steps)
        def _():
            den_copy(j + 1).wait()

        mat_copy(j).wait()

        @pl.when(j + 2 < steps)
        def _():
            den_copy(j + 2).start()
            mat_copy(j + 2).start()

        start = pl.multiple_of(j * CB, CB)
        left = pl.multiple_of(jnp.maximum(start - LANES, 0), LANES)
        right = pl.multiple_of(jnp.minimum(start + CB, columns - LANES), LANES)
        inside_left = jnp.where(j == 0, 0.0, 1.0).astype(jnp.bfloat16)
        inside_right = jnp.where(j == steps - 1, 0.0, 1.0).astype(jnp.bfloat16)

        def fill(r):
            for z in range(ghost):
                for c in range(PER):
                    cols = pl.ds(start + c * LANES, LANES)
                    if r == 0 and 0 < z < ghost - 1:
                        full[z, c, SUB - 1 : SUB, :] = low_ref[z - 1 : z, cols].astype(jnp.float32)
                    full[z, c, pl.ds(SUB + r * CHUNK, CHUNK), :] = den[z, pl.ds(r * CHUNK, CHUNK), cols].astype(jnp.float32)
                    if r == rows // CHUNK - 1 and 0 < z < ghost - 1:
                        full[z, c, SUB + rows : SUB + rows + 1, :] = high_ref[z - 1 : z, cols].astype(jnp.float32)

        def across(r):
            spots = pl.ds(r * CHUNK, CHUNK)
            window = jnp.concatenate(
                [
                    den[1:-1, spots, pl.ds(left, LANES)] * inside_left,
                    den[1:-1, spots, pl.ds(start, CB)],
                    den[1:-1, spots, pl.ds(right, LANES)] * inside_right,
                ],
                axis=-1,
            )
            diff[:, spots, :] = jnp.dot(
                window.reshape(slices * CHUNK, CB + 2 * LANES), band[...], preferred_element_type=jnp.float32
            ).reshape(slices, CHUNK, CB)

        def shade_tile(base, c):
            spots = pl.ds(base, SUB)
            through = jnp.ones((SUB, LANES), jnp.float32)
            depth = jnp.zeros((SUB, LANES), jnp.float32)
            sums = [jnp.zeros((SUB, LANES), jnp.float32) for _ in range(3)]
            for z in range(slices):
                rho = full[z + 1, c, pl.ds(base + SUB, SUB), :]
                dz = full[z + 2, c, pl.ds(base + SUB, SUB), :] - full[z, c, pl.ds(base + SUB, SUB), :]
                dy = full[z + 1, c, pl.ds(base + SUB + 1, SUB), :] - full[z + 1, c, pl.ds(base + SUB - 1, SUB), :]
                dx = diff[z, spots, pl.ds(c * LANES, LANES)]
                lit = dx + (light_y / light_x) * dy + (light_z / light_x) * dz
                bend = lax.rsqrt(4.0 + dx * dx + dy * dy + dz * dz)
                shade = ambient / (diffuse * light_x) + lit * bend
                kind = mat[z, spots, pl.ds(start + c * LANES, LANES)]
                upper = kind >= SUB
                index = kind & (SUB - 1)
                depth = depth + pick(tables[0], tables[1], index, upper) * (rho * (1.0 / (1.0 + rho)))
                after = jnp.exp2(depth)
                weight = (through - after) * shade
                through = after
                for channel in range(3):
                    if channel < LANE_TABLES:
                        color = lane_entries(tables[2 + 2 * channel], kind)
                    else:
                        color = pick(tables[2 + 2 * channel], tables[3 + 2 * channel], index, upper)
                    sums[channel] = sums[channel] + weight * color
            red, green, blue = (quantize(jnp.log2(value), LOG_LOW, LOG_STEP) for value in sums)
            deep = quantize(depth, 0.0, -TAU_STEP)
            spot = base * stride + j * PER + c
            out_ref[pl.ds(spot, SUB, stride=stride), :] = (red << 16) | green
            out_ref[pl.ds(spot + blocks, SUB, stride=stride), :] = (blue << 16) | deep

        chunks = rows // CHUNK
        fill(0)
        across(0)
        for r in range(chunks):
            if r + 1 < chunks:
                fill(r + 1)
                across(r + 1)
            for base in range(r * CHUNK, (r + 1) * CHUNK, SUB):
                for c in range(PER):
                    shade_tile(base, c)
        return carry

    den_copy(0).wait()
    lax.fori_loop(0, steps, shade_columns, 0)


def shade_bricks(density, low, high, material, color_table, extinction):
    table, band = prepare(color_table, extinction)
    ghost, rows, columns = density.shape
    slices = material.shape[0]
    steps = columns // CB
    blocks = columns // LANES
    return pl.pallas_call(
        shade_kernel,
        in_specs=[
            pl.BlockSpec(memory_space=pltpu.HBM),
            pl.BlockSpec(memory_space=pltpu.VMEM),
            pl.BlockSpec(memory_space=pltpu.VMEM),
            pl.BlockSpec(memory_space=pltpu.HBM),
            pl.BlockSpec(memory_space=pltpu.VMEM),
            pl.BlockSpec(memory_space=pltpu.VMEM),
        ],
        out_specs=pl.BlockSpec(memory_space=pltpu.VMEM),
        out_shape=jax.ShapeDtypeStruct((rows * 2 * blocks, LANES), jnp.int32),
        scratch_shapes=[
            pltpu.VMEM((ghost, rows, columns), jnp.bfloat16),
            pltpu.VMEM((slices, rows, columns), jnp.int32),
            pltpu.VMEM((ghost, PER, rows + 2 * SUB, LANES), jnp.float32),
            pltpu.VMEM((slices, rows, CB), jnp.float32),
            pltpu.SemaphoreType.DMA((steps,)),
            pltpu.SemaphoreType.DMA((steps,)),
        ],
        compiler_params=pltpu.CompilerParams(vmem_limit_bytes=VLIM << 20),
    )(density, low, high, material, table, band)


def end_rows_kernel(den_hbm, first_ref, last_ref, top, bottom, sem):
    slices, tile = top.shape[0], top.shape[1]
    rows = den_hbm.shape[1]
    copies = [
        pltpu.make_async_copy(den_hbm.at[1 : 1 + slices, start : start + tile, :], held, sem.at[i])
        for i, (start, held) in enumerate(((0, top), (rows - tile, bottom)))
    ]
    for copy in copies:
        copy.start()
    for copy in copies:
        copy.wait()
    for z in range(slices):
        first_ref[z : z + 1, :] = top[z, :1, :]
        last_ref[z : z + 1, :] = bottom[z, tile - 1 :, :]


def end_rows(density):
    ghost, rows, columns = density.shape
    row = jax.ShapeDtypeStruct((ghost - 2, columns), density.dtype)
    vmem = pl.BlockSpec(memory_space=pltpu.VMEM)
    tile = pltpu.VMEM((ghost - 2, SUB, columns), density.dtype)
    return pl.pallas_call(
        end_rows_kernel,
        in_specs=[pl.BlockSpec(memory_space=pltpu.HBM)],
        out_specs=[vmem, vmem],
        out_shape=[row, row],
        scratch_shapes=[tile, tile, pltpu.SemaphoreType.DMA((2,))],
        compiler_params=pltpu.CompilerParams(vmem_limit_bytes=VLIM << 20),
    )(density)


def blend_kernel(order_ref, part_ref, out_ref, place, image):
    bricks, rows, pairs, blocks, lanes = part_ref.shape
    for brick in range(bricks):
        place[order_ref[brick]] = brick
    spots = [(row, group) for row in range(rows) for group in range(0, blocks, SUB)]

    def walk(rank, carry):
        brick = place[rank]
        after = []
        for (row, group), (front, red, green, blue) in zip(spots, carry):
            first = part_ref[brick, row, 0, group : group + SUB, :]
            second = part_ref[brick, row, 1, group : group + SUB, :]
            low = LOG_LOW - front

            def seen(code):
                return jnp.exp2(code.astype(jnp.float32) * LOG_STEP + low)

            red = red + seen(lax.shift_right_logical(first, 16))
            green = green + seen(first & 0xFFFF)
            blue = blue + seen(lax.shift_right_logical(second, 16))
            front = front + (second & 0xFFFF).astype(jnp.float32) * TAU_STEP
            after.append((front, red, green, blue))
        return tuple(after)

    zero = jnp.zeros((SUB, lanes), jnp.float32)
    sums = lax.fori_loop(0, bricks, walk, tuple((zero,) * 4 for _ in spots), unroll=16)
    for (row, group), (front, red, green, blue) in zip(spots, sums):
        for channel, value in enumerate((red, green, blue, 1.0 - jnp.exp2(-front))):
            image[pl.ds((row * 4 + channel) * blocks + group, SUB), :] = value
    for row in range(rows):
        for block in range(blocks):
            out_ref[row, :, pl.ds(block * lanes, lanes)] = image[pl.ds(row * 4 * blocks + block, 4, stride=blocks), :]


def blend(order, part):
    bricks, rows, pairs, blocks, lanes = part.shape
    return pl.pallas_call(
        blend_kernel,
        in_specs=[pl.BlockSpec(memory_space=pltpu.SMEM), pl.BlockSpec(memory_space=pltpu.VMEM)],
        out_specs=pl.BlockSpec(memory_space=pltpu.VMEM),
        out_shape=jax.ShapeDtypeStruct((rows, 4, blocks * lanes), jnp.float32),
        scratch_shapes=[pltpu.SMEM((bricks,), jnp.int32), pltpu.VMEM((rows * 4 * blocks, lanes), jnp.float32)],
        compiler_params=pltpu.CompilerParams(vmem_limit_bytes=8 << 20),
    )(order, part)


def body(density, material, order, color_table, extinction):
    count = lax.axis_size("screen")
    rows, columns = density.shape[1], density.shape[2]
    bricks = lax.axis_size("depth")
    forward = [(i, i + 1) for i in range(count - 1)]
    backward = [(target, source) for source, target in forward]
    first, last = end_rows(density)
    low = lax.ppermute(last, "screen", forward)
    high = lax.ppermute(first, "screen", backward)
    coded = shade_bricks(density, low, high, material, color_table.T, extinction)
    blocks = columns // LANES
    strip = rows // bricks
    parts = coded.reshape(bricks, strip * 2 * blocks, LANES)
    parts = lax.all_to_all(parts, "depth", split_axis=0, concat_axis=0, tiled=True)
    image = blend(order, parts.reshape(bricks, strip, 2, blocks, LANES))
    return image.transpose(1, 0, 2)


def solution(mesh):
    placed = (P("depth", "screen", None), P("depth", "screen", None), P(), P(), P())
    return jax.shard_map(
        body,
        mesh=mesh,
        in_specs=placed,
        out_specs=P(None, ("screen", "depth"), None),
        check_vma=False,
    )
```

```python
import functools
import math

import jax
import jax.numpy as jnp
from jax import lax
from jax.experimental import pallas as pl
from jax.experimental.pallas import tpu as pltpu
from jax.sharding import PartitionSpec as P

light_x = 0.48
light_y = 0.6
light_z = 0.64
ambient = 0.55
diffuse = 0.45

LANES = 128
SUB = 8
CB = 256
PER = CB // LANES
CHUNK = 32
VLIM = 52
LANE_TABLES = 2
LOG2E = math.log2(math.e)

SLICES = 8
TAU_TOP = SLICES * 0.0390625 * (10.0 / 11.0) * LOG2E * 1.001
LOG_TOP = 0.0
LOG_LOW = -14.0
LEVELS = 65535.0
TAU_STEP = TAU_TOP / LEVELS
LOG_STEP = (LOG_TOP - LOG_LOW) / LEVELS


def quantize(value, low, step):
    return (value * (1.0 / step) + (0.5 - low / step)).astype(jnp.int32)


def entries_at(table, index):
    numbers = lax.GatherDimensionNumbers(
        offset_dims=(),
        collapsed_slice_dims=(0,),
        start_index_map=(0,),
        operand_batching_dims=(1,),
        start_indices_batching_dims=(1,),
    )
    return lax.gather(
        table, index[..., None], numbers, (1, 1), mode=lax.GatherScatterMode.PROMISE_IN_BOUNDS
    )


def lane_entries(table, index):
    numbers = lax.GatherDimensionNumbers(
        offset_dims=(),
        collapsed_slice_dims=(1,),
        start_index_map=(1,),
        operand_batching_dims=(0,),
        start_indices_batching_dims=(0,),
    )
    return lax.gather(
        table, index[..., None], numbers, (1, 1), mode=lax.GatherScatterMode.PROMISE_IN_BOUNDS
    )


def pick(low_table, high_table, index, upper):
    return jnp.where(upper, entries_at(high_table, index), entries_at(low_table, index))


def prepare_kernel(color_ref, ext_ref, table, band):
    source = lax.broadcasted_iota(jnp.int32, (2 * SUB, LANES), 0)
    target = lax.broadcasted_iota(jnp.int32, (2 * SUB, LANES), 1)
    for top in range(0, CB + 2 * LANES, 2 * SUB):
        for side in range(0, CB, LANES):
            shift = (source + (top - LANES)) - (target + side)
            tile = (shift == 1).astype(jnp.float32) - (shift == -1).astype(jnp.float32)
            band[top : top + 2 * SUB, side : side + LANES] = tile.astype(jnp.bfloat16)
    lane = lax.broadcasted_iota(jnp.int32, (SUB, LANES), 1)
    for channel in range(LANE_TABLES):
        table[3 + 2 * channel] = jnp.zeros((SUB, LANES), jnp.float32)
        spread = jnp.zeros((SUB, LANES), jnp.float32)
        for entry in range(2 * SUB):
            spread = jnp.where(lane == entry, (diffuse * light_x) * color_ref[channel, entry], spread)
        table[2 + 2 * channel] = spread
    for entry in range(SUB):
        for half in range(2):
            spot = entry + half * SUB
            table[half, entry : entry + 1, :] = jnp.full((1, LANES), -LOG2E * ext_ref[spot], jnp.float32)
            for channel in range(LANE_TABLES, 3):
                scale = (diffuse * light_x) * color_ref[channel, spot]
                table[2 + 2 * channel + half, entry : entry + 1, :] = jnp.full((1, LANES), scale, jnp.float32)


def prepare(color_table, extinction):
    smem = pl.BlockSpec(memory_space=pltpu.SMEM)
    vmem = pl.BlockSpec(memory_space=pltpu.VMEM)
    return pl.pallas_call(
        prepare_kernel,
        in_specs=[smem, smem],
        out_specs=[vmem, vmem],
        out_shape=[
            jax.ShapeDtypeStruct((8, SUB, LANES), jnp.float32),
            jax.ShapeDtypeStruct((CB + 2 * LANES, CB), jnp.bfloat16),
        ],
        compiler_params=pltpu.CompilerParams(vmem_limit_bytes=VLIM << 20),
    )(color_table, extinction)


def shade_kernel(den_hbm, high_ref, low_ref, mat_hbm, table, band, out_ref, den, mat, full, diff, den_sem, mat_sem):
    ghost, rows, columns = den.shape
    slices = ghost - 2
    steps = columns // CB
    blocks = columns // LANES
    stride = 2 * blocks

    def den_copy(j):
        cols = pl.ds(pl.multiple_of(j * CB, CB), CB)
        return pltpu.make_async_copy(den_hbm.at[:, :, cols], den.at[:, :, cols], den_sem.at[j])

    def mat_copy(j):
        cols = pl.ds(pl.multiple_of(j * CB, CB), CB)
        return pltpu.make_async_copy(mat_hbm.at[:, :, cols], mat.at[:, :, cols], mat_sem.at[j])

    den_copy(0).start()
    mat_copy(0).start()
    den_copy(1).start()
    mat_copy(1).start()

    tables = [table[i] for i in range(8)]

    def shade_columns(j, carry):
        @pl.when(j + 1 < steps)
        def _():
            den_copy(j + 1).wait()

        mat_copy(j).wait()

        @pl.when(j + 2 < steps)
        def _():
            den_copy(j + 2).start()
            mat_copy(j + 2).start()

        start = pl.multiple_of(j * CB, CB)
        left = pl.multiple_of(jnp.maximum(start - LANES, 0), LANES)
        right = pl.multiple_of(jnp.minimum(start + CB, columns - LANES), LANES)
        inside_left = jnp.where(j == 0, 0.0, 1.0).astype(jnp.bfloat16)
        inside_right = jnp.where(j == steps - 1, 0.0, 1.0).astype(jnp.bfloat16)

        def fill(r):
            for z in range(ghost):
                for c in range(PER):
                    cols = pl.ds(start + c * LANES, LANES)
                    if r == 0 and 0 < z < ghost - 1:
                        full[z, c, SUB - 1 : SUB, :] = low_ref[z - 1 : z, cols].astype(jnp.float32)
                    full[z, c, pl.ds(SUB + r * CHUNK, CHUNK), :] = den[z, pl.ds(r * CHUNK, CHUNK), cols].astype(jnp.float32)
                    if r == rows // CHUNK - 1 and 0 < z < ghost - 1:
                        full[z, c, SUB + rows : SUB + rows + 1, :] = high_ref[z - 1 : z, cols].astype(jnp.float32)

        def across(r):
            spots = pl.ds(r * CHUNK, CHUNK)
            window = jnp.concatenate(
                [
                    den[1:-1, spots, pl.ds(left, LANES)] * inside_left,
                    den[1:-1, spots, pl.ds(start, CB)],
                    den[1:-1, spots, pl.ds(right, LANES)] * inside_right,
                ],
                axis=-1,
            )
            diff[:, spots, :] = jnp.dot(
                window.reshape(slices * CHUNK, CB + 2 * LANES), band[...], preferred_element_type=jnp.float32
            ).reshape(slices, CHUNK, CB)

        def shade_tile(base, c):
            spots = pl.ds(base, SUB)
            through = jnp.ones((SUB, LANES), jnp.float32)
            depth = jnp.zeros((SUB, LANES), jnp.float32)
            sums = [jnp.zeros((SUB, LANES), jnp.float32) for _ in range(3)]
            for z in range(slices):
                rho = full[z + 1, c, pl.ds(base + SUB, SUB), :]
                dz = full[z + 2, c, pl.ds(base + SUB, SUB), :] - full[z, c, pl.ds(base + SUB, SUB), :]
                dy = full[z + 1, c, pl.ds(base + SUB + 1, SUB), :] - full[z + 1, c, pl.ds(base + SUB - 1, SUB), :]
                dx = diff[z, spots, pl.ds(c * LANES, LANES)]
                lit = dx + (light_y / light_x) * dy + (light_z / light_x) * dz
                bend = lax.rsqrt(4.0 + dx * dx + dy * dy + dz * dz)
                shade = ambient / (diffuse * light_x) + lit * bend
                kind = mat[z, spots, pl.ds(start + c * LANES, LANES)]
                upper = kind >= SUB
                index = kind & (SUB - 1)
                depth = depth + pick(tables[0], tables[1], index, upper) * (rho * (1.0 / (1.0 + rho)))
                after = jnp.exp2(depth)
                weight = (through - after) * shade
                through = after
                for channel in range(3):
                    if channel < LANE_TABLES:
                        color = lane_entries(tables[2 + 2 * channel], kind)
                    else:
                        color = pick(tables[2 + 2 * channel], tables[3 + 2 * channel], index, upper)
                    sums[channel] = sums[channel] + weight * color
            red, green, blue = (quantize(jnp.log2(value), LOG_LOW, LOG_STEP) for value in sums)
            deep = quantize(depth, 0.0, -TAU_STEP)
            spot = base * stride + j * PER + c
            out_ref[pl.ds(spot, SUB, stride=stride), :] = (red << 16) | green
            out_ref[pl.ds(spot + blocks, SUB, stride=stride), :] = (blue << 16) | deep

        chunks = rows // CHUNK
        fill(0)
        across(0)
        for r in range(chunks):
            if r + 1 < chunks:
                fill(r + 1)
                across(r + 1)
            for base in range(r * CHUNK, (r + 1) * CHUNK, SUB):
                for c in range(PER):
                    shade_tile(base, c)
        return carry

    den_copy(0).wait()
    lax.fori_loop(0, steps, shade_columns, 0)


def shade_bricks(density, low, high, material, color_table, extinction):
    table, band = prepare(color_table, extinction)
    ghost, rows, columns = density.shape
    slices = material.shape[0]
    steps = columns // CB
    blocks = columns // LANES
    return pl.pallas_call(
        shade_kernel,
        in_specs=[
            pl.BlockSpec(memory_space=pltpu.HBM),
            pl.BlockSpec(memory_space=pltpu.VMEM),
            pl.BlockSpec(memory_space=pltpu.VMEM),
            pl.BlockSpec(memory_space=pltpu.HBM),
            pl.BlockSpec(memory_space=pltpu.VMEM),
            pl.BlockSpec(memory_space=pltpu.VMEM),
        ],
        out_specs=pl.BlockSpec(memory_space=pltpu.VMEM),
        out_shape=jax.ShapeDtypeStruct((rows * 2 * blocks, LANES), jnp.int32),
        scratch_shapes=[
            pltpu.VMEM((ghost, rows, columns), jnp.bfloat16),
            pltpu.VMEM((slices, rows, columns), jnp.int32),
            pltpu.VMEM((ghost, PER, rows + 2 * SUB, LANES), jnp.float32),
            pltpu.VMEM((slices, rows, CB), jnp.float32),
            pltpu.SemaphoreType.DMA((steps,)),
            pltpu.SemaphoreType.DMA((steps,)),
        ],
        compiler_params=pltpu.CompilerParams(vmem_limit_bytes=VLIM << 20),
    )(density, high, low, material, table, band)


def end_rows_kernel(den_hbm, first_ref, last_ref, top, bottom, sem):
    slices, tile = top.shape[0], top.shape[1]
    rows = den_hbm.shape[1]
    copies = [
        pltpu.make_async_copy(den_hbm.at[1 : 1 + slices, start : start + tile, :], held, sem.at[i])
        for i, (start, held) in enumerate(((0, top), (rows - tile, bottom)))
    ]
    for copy in copies:
        copy.start()
    for copy in copies:
        copy.wait()
    for z in range(slices):
        first_ref[z : z + 1, :] = top[z, :1, :]
        last_ref[z : z + 1, :] = bottom[z, tile - 1 :, :]


def end_rows(density):
    ghost, rows, columns = density.shape
    row = jax.ShapeDtypeStruct((ghost - 2, columns), density.dtype)
    vmem = pl.BlockSpec(memory_space=pltpu.VMEM)
    tile = pltpu.VMEM((ghost - 2, SUB, columns), density.dtype)
    return pl.pallas_call(
        end_rows_kernel,
        in_specs=[pl.BlockSpec(memory_space=pltpu.HBM)],
        out_specs=[vmem, vmem],
        out_shape=[row, row],
        scratch_shapes=[tile, tile, pltpu.SemaphoreType.DMA((2,))],
        compiler_params=pltpu.CompilerParams(vmem_limit_bytes=VLIM << 20),
    )(density)


def blend_kernel(order_ref, part_ref, out_ref, place, image):
    bricks, rows, pairs, blocks, lanes = part_ref.shape
    for brick in range(bricks):
        place[order_ref[brick]] = brick
    spots = [(row, group) for row in range(rows) for group in range(0, blocks, SUB)]

    def walk(rank, carry):
        brick = place[rank]
        after = []
        for (row, group), (front, red, green, blue) in zip(spots, carry):
            first = part_ref[brick, row, 0, group : group + SUB, :]
            second = part_ref[brick, row, 1, group : group + SUB, :]
            low = LOG_LOW - front

            def seen(code):
                return jnp.exp2(code.astype(jnp.float32) * LOG_STEP + low)

            red = red + seen(lax.shift_right_logical(first, 16))
            green = green + seen(first & 0xFFFF)
            blue = blue + seen(lax.shift_right_logical(second, 16))
            front = front + (second & 0xFFFF).astype(jnp.float32) * TAU_STEP
            after.append((front, red, green, blue))
        return tuple(after)

    zero = jnp.zeros((SUB, lanes), jnp.float32)
    sums = lax.fori_loop(0, bricks, walk, tuple((zero,) * 4 for _ in spots), unroll=16)
    for (row, group), (front, red, green, blue) in zip(spots, sums):
        for channel, value in enumerate((red, green, blue, 1.0 - jnp.exp2(-front))):
            image[pl.ds((row * 4 + channel) * blocks + group, SUB), :] = value
    for row in range(rows):
        for block in range(blocks):
            out_ref[row, :, pl.ds(block * lanes, lanes)] = image[pl.ds(row * 4 * blocks + block, 4, stride=blocks), :]


def blend(order, part):
    bricks, rows, pairs, blocks, lanes = part.shape
    return pl.pallas_call(
        blend_kernel,
        in_specs=[pl.BlockSpec(memory_space=pltpu.SMEM), pl.BlockSpec(memory_space=pltpu.VMEM)],
        out_specs=pl.BlockSpec(memory_space=pltpu.VMEM),
        out_shape=jax.ShapeDtypeStruct((rows, 4, blocks * lanes), jnp.float32),
        scratch_shapes=[pltpu.SMEM((bricks,), jnp.int32), pltpu.VMEM((rows * 4 * blocks, lanes), jnp.float32)],
        compiler_params=pltpu.CompilerParams(vmem_limit_bytes=8 << 20),
    )(order, part)


def body(density, material, order, color_table, extinction):
    count = lax.axis_size("screen")
    rows, columns = density.shape[1], density.shape[2]
    bricks = lax.axis_size("depth")
    forward = [(i, i + 1) for i in range(count - 1)]
    backward = [(target, source) for source, target in forward]
    first, last = end_rows(density)
    low = lax.ppermute(last, "screen", forward)
    high = lax.ppermute(first, "screen", backward)
    coded = shade_bricks(density, low, high, material, color_table.T, extinction)
    blocks = columns // LANES
    strip = rows // bricks
    parts = coded.reshape(bricks, strip * 2 * blocks, LANES)
    parts = lax.all_to_all(parts, "depth", split_axis=0, concat_axis=0, tiled=True)
    image = blend(order, parts.reshape(bricks, strip, 2, blocks, LANES))
    return image.transpose(1, 0, 2)


def solution(mesh):
    placed = (P("depth", "screen", None), P("depth", "screen", None), P(), P(), P())
    return jax.shard_map(
        body,
        mesh=mesh,
        in_specs=placed,
        out_specs=P(None, ("screen", "depth"), None),
        check_vma=False,
    )
```
